32 devices in a mesh: slab: 4 (over x, core), panel: 8 (over z, y).
Axes of the slice: x: 2, y: 2, z: 4, core: 2. Of those that a mesh axis runs over, the one named last changes fastest.
Arguments:
- ranges: float32 [4, 4, 1024, 1024], P('slab', None, 'panel'), may hold values from -1.5 to 1.5
- pattern: int32 [4, 4, 16, 16], P('slab'), may hold values 0 or 1
Outputs:
- combined: float32 [4, 4, 1024, 1024], P('slab', None, 'panel')
The draws below stay inside these ranges and needn't reach their ends.
All inputs are finite; a program needn't handle non-finite values. No bound on the sum of `pattern` on one device may be relied on, other than what follows from the above.
Results may differ from the reference program's by a relative error of at most 0.01.
Values may be sent and summed in bfloat16 or wider, within the bound.
A program may use at most 64 MiB of HBM per device.

```python
import math
import jax
import jax.numpy as jnp
from jax import lax

M = 1024
BLK = 64
NS_ITERS = 2
LEVELS = 2
GROUPS = 4
NB = 16


def draw_ranges(key, part):
    noise_key = jax.random.fold_in(key, 0)
    sign_key = jax.random.fold_in(key, 1)
    size_key = jax.random.fold_in(key, 2)
    turn_key = jax.random.fold_in(key, 4)
    spread_vals = jnp.clip(jax.random.normal(noise_key, (GROUPS, 4, M, M), jnp.float32), -6.0, 6.0)
    off_part = spread_vals * (0.25 / math.sqrt(M))
    reflect_sign = jnp.where(jax.random.bernoulli(sign_key, 0.5, (GROUPS, M)), 1.0, -1.0)
    carry_sign = jnp.where(jax.random.bernoulli(turn_key, 0.5, (GROUPS, M)), 1.0, -1.0)
    reflect = jax.random.uniform(size_key, (GROUPS, M), jnp.float32, 0.4, 0.7)
    carry = jnp.sqrt(1.0 - reflect * reflect)
    diag_vals = jnp.stack([reflect_sign * reflect, carry_sign * carry, carry_sign * carry, -reflect_sign * reflect], axis=1)
    diagonal = jnp.eye(M, dtype=jnp.float32)[None, None, :, :] * diag_vals[:, :, :, None]
    return (off_part + diagonal).astype(jnp.float32)


def set_ends(values, own_key, least, top_value):
    extent = values.shape
    spot = [jax.random.randint(jax.random.fold_in(own_key, axis), (), 0, extent[axis]) for axis in range(len(extent))]
    values = values.at[tuple(spot)].set(least)
    longest = extent.index(max(extent))
    spot[longest] = (spot[longest] + 1) % extent[longest]
    return values.at[tuple(spot)].set(top_value)


def setup_inputs(seed: int = 0) -> dict:
    arg_keys = jax.random.split(jax.random.key(seed), 3)
    return {
        "ranges": draw_ranges(jax.random.fold_in(arg_keys[2], 71), 0),
        "pattern": set_ends((jax.random.randint(arg_keys[1], (GROUPS, 4, NB, NB), 0, 4) < 3).astype(jnp.int32), jax.random.fold_in(arg_keys[1], 1), 0, 1),
    }


def to_half(values):
    return values.astype(jnp.bfloat16)


def multiply(left, right):
    return jnp.dot(to_half(left), to_half(right), preferred_element_type=jnp.float32)


def star(head, tail):
    head_top, head_up, head_down, head_bottom = head[0], head[1], head[2], head[3]
    tail_top, tail_up, tail_down, tail_bottom = tail[0], tail[1], tail[2], tail[3]
    identity = jnp.eye(M, dtype=jnp.float32)
    loop_term = multiply(tail_top, head_bottom)
    loop_kept = lax.optimization_barrier(to_half(loop_term)).astype(jnp.float32)
    defect = identity - loop_kept
    guess = identity + loop_kept
    for newton_step in range(2, NS_ITERS + 1):
        guess = 2.0 * guess - multiply(multiply(guess, defect), guess)
    lifted = multiply(head_up, guess)
    joint_up = multiply(lifted, tail_up)
    bounce = multiply(tail_top, head_down)
    joint_top = head_top + multiply(lifted, bounce)
    reach = multiply(tail_down, head_bottom)
    through = multiply(reach, guess)
    joint_down = multiply(tail_down, head_down) + multiply(through, bounce)
    joint_bottom = tail_bottom + multiply(reach, tail_up) + multiply(multiply(through, loop_term), tail_up)
    return jnp.stack([joint_top, joint_up, joint_down, joint_bottom])


def reference(ranges, pattern):
    block_mask = jnp.repeat(jnp.repeat(pattern.astype(jnp.float32), BLK, axis=2), BLK, axis=3)
    merged = [ranges[group_id] * block_mask[group_id] for group_id in range(GROUPS)]
    for tree_level in range(LEVELS):
        span_size = 2 ** tree_level
        outcome = list(merged)
        for low_group in range(GROUPS):
            if (low_group // span_size) % 2 == 0:
                result = star(merged[low_group], merged[low_group + span_size])
                outcome[low_group] = result
                outcome[low_group + span_size] = result
        merged = outcome
    return jnp.stack(merged)
```

```python
import functools
import jax
import jax.numpy as jnp
from jax import lax
from jax.experimental import pallas as pl
from jax.experimental.pallas import tpu as pltpu
from jax.sharding import PartitionSpec as P

BLK = 64
TILE = 256
MESH = pl.DeviceIdType.MESH


def kernel(outer, inner, counts, first_ref, second_ref, left_ref, add_ref, own_ref, other_ref,
           right, swap, base, front, mid, recv_sem, send_sem, swap_recv, swap_send, local_sem, last_recv, last_send):
    rows, width = left_ref.shape
    slab = lax.axis_index("slab")
    panel = lax.axis_index("panel")
    core = slab % 2
    side = (slab // 2) % 2
    sibling = slab + 1 - 2 * core
    partner = slab + 2 - 4 * side
    out_pos = panel // inner
    in_pos = panel % inner

    def flip(value, bits):
        result = value
        for bit in range(6):
            if bits >> bit & 1:
                result = result + (1 << bit) * (1 - 2 * ((value // (1 << bit)) % 2))
        return result

    outer_peers = [flip(out_pos, i) * inner + in_pos for i in range(1, outer)]
    inner_bits = range(1, inner)

    barrier = pltpu.get_barrier_semaphore()
    friends = [(slab, p) for p in outer_peers]
    friends += [(slab, out_pos * inner + flip(in_pos, j)) for j in inner_bits]
    friends += [(sibling, panel), (partner, panel)]
    for friend in friends:
        pl.semaphore_signal(barrier, inc=1, device_id=friend, device_id_type=MESH)
    pl.semaphore_wait(barrier, len(friends))

    sent = []
    used = [0]

    def place(level, kind, owner, p):
        return right.at[level, kind, owner, pl.ds(pl.multiple_of(p * rows, rows), rows), :]

    def push(level, kind, src, p, target):
        spot = used[0]
        used[0] += 1
        copy = pltpu.make_async_remote_copy(
            src_ref=src, dst_ref=place(level, kind, core, p), send_sem=send_sem.at[spot],
            recv_sem=recv_sem.at[level, kind, core, p], device_id=target, device_id_type=MESH)
        copy.start()
        sent.append(copy)

    def arrive(level, kind, owner, p):
        spot = place(level, kind, owner, p)
        pltpu.make_async_remote_copy(
            src_ref=spot, dst_ref=spot, send_sem=send_sem.at[0],
            recv_sem=recv_sem.at[level, kind, owner, p], device_id=(sibling, panel), device_id_type=MESH).wait_recv()

    def to_inner(level, kind, src, p):
        for j in inner_bits:
            push(level, kind, src, p, (slab, out_pos * inner + flip(in_pos, j)))

    def to_sibling(level, kind, src, p):
        push(level, kind, src, p, (sibling, panel))

    def open_gather(level, kind, src):
        copy = pltpu.make_async_copy(src, place(level, kind, core, panel), local_sem.at[level, kind])
        copy.start()
        for p in outer_peers:
            push(level, kind, src, panel, (slab, p))
        to_inner(level, kind, src, panel)
        to_sibling(level, kind, src, panel)
        return copy

    def relay_outer(level, kind, i):
        p = outer_peers[i]
        arrive(level, kind, core, p)
        to_inner(level, kind, place(level, kind, core, p), p)
        to_sibling(level, kind, place(level, kind, core, p), p)

    def relay_inner(level, kind):
        for i in range(outer):
            for j in inner_bits:
                p = flip(out_pos, i) * inner + flip(in_pos, j)
                arrive(level, kind, core, p)
                to_sibling(level, kind, place(level, kind, core, p), p)

    def settle(level, kind, copy):
        for i in range(outer):
            for j in range(inner):
                arrive(level, kind, 1 - core, flip(out_pos, i) * inner + flip(in_pos, j))
        copy.wait()

    def product(left, factor, emit):
        @pl.loop(0, width // TILE)
        def _(step):
            cols = pl.ds(pl.multiple_of(step * TILE, TILE), TILE)
            emit(cols, jnp.dot(left[...], factor[:, cols], preferred_element_type=jnp.float32))

    def keep(ref):
        def emit(cols, value):
            ref[:, cols] = value.astype(ref.dtype)
        return emit

    def keep_sum(ref, extra):
        def emit(cols, value):
            ref[:, cols] = (extra[:, cols].astype(jnp.float32) + value).astype(ref.dtype)
        return emit

    is_tail = core == 1

    def merge(level, first, second, left, add, outs, after_diag):
        copies = [open_gather(level, 0, first), open_gather(level, 1, second())]
        for i in range(outer - 1):
            relay_outer(level, 0, i)
        relay_inner(level, 0)
        settle(level, 0, copies[0])
        top = right.at[level, 0, 1 - level]
        bottom = right.at[level, 0, level]

        @pl.when(is_tail)
        def _():
            product(left, bottom, keep(base))

        @pl.when(core == 0)
        def _():
            base[...] = left[...]

        pending = list(range(outer - 1))
        for turn in range(3):
            product(base if turn == 0 else front, top, keep(mid))
            if pending:
                relay_outer(level, 1, pending.pop(0))
            product(mid, bottom, keep_sum(front, base))
        for i in pending:
            relay_outer(level, 1, i)
        product(front, top, keep(mid))
        relay_inner(level, 1)

        @pl.when(is_tail)
        def _():
            front[...] = (left[...].astype(jnp.float32) + mid[...].astype(jnp.float32)).astype(front.dtype)
            product(mid, bottom, keep_sum(base, base))

        @pl.when(core == 0)
        def _():
            base[...] = mid[...]

        settle(level, 1, copies[1])
        mine = right.at[level, 1, core]
        theirs = right.at[level, 1, 1 - core]
        diag_factor, side_factor = (mine, theirs) if level == 0 else (theirs, mine)
        product(base, diag_factor, keep_sum(outs[0], add))
        after_diag()
        product(front, side_factor, keep(outs[1]))

    gives = lax.rem(side + core, 2)
    slot = 1 - gives

    def swap_copy(kind, which):
        return pltpu.make_async_remote_copy(
            src_ref=swap.at[which, kind], dst_ref=swap.at[which, kind], send_sem=swap_send.at[kind],
            recv_sem=swap_recv.at[kind], device_id=(partner, panel), device_id_type=MESH)

    merge(0, first_ref, lambda: second_ref, left_ref, add_ref,
          (swap.at[slot, 0], swap.at[slot, 1]), lambda: swap_copy(0, slot).start())
    swap_copy(1, slot).start()
    swap_copy(0, gives).wait_recv()

    def swap_second():
        swap_copy(1, gives).wait_recv()
        return swap.at[0, 1]

    def last_copy(kind):
        return pltpu.make_async_remote_copy(
            src_ref=own_ref.at[kind], dst_ref=other_ref.at[kind], send_sem=last_send.at[kind],
            recv_sem=last_recv.at[kind], device_id=(sibling, panel), device_id_type=MESH)

    merge(1, swap.at[0, 0], swap_second, swap.at[1, 1], swap.at[1, 0],
          (own_ref.at[0], own_ref.at[1]), lambda: last_copy(0).start())
    last_copy(1).start()
    for kind in range(2):
        swap_copy(kind, slot).wait_send()
    for copy in sent:
        copy.wait_send()
    for kind in range(2):
        last_copy(kind).wait()
    assert used[0] == counts


def body(panels, ranges, pattern):
    blocks = ranges[0]
    rows, width = blocks.shape[1:]
    count = pattern.shape[2]
    core = lax.axis_index("slab") % 2
    row_start = lax.axis_index("panel") * rows
    row_ids = row_start + jnp.arange(rows, dtype=jnp.int32)
    col_ids = jnp.arange(width, dtype=jnp.int32)
    block_ids = jnp.arange(count, dtype=jnp.int32)
    row_pick = (row_ids[:, None] // BLK == block_ids[None, :]).astype(jnp.float32)
    col_pick = (block_ids[:, None] == col_ids[None, :] // BLK).astype(jnp.float32)
    mask = jnp.einsum("mi,gij,jc->gmc", row_pick, pattern[0].astype(jnp.float32), col_pick)
    masked = blocks * mask
    half = masked.astype(jnp.bfloat16)
    head = core == 0
    first = jnp.where(head, half[3], half[0])
    second = jnp.where(head, half[2], half[1])
    left = jnp.where(head, half[1], half[2])
    add = jnp.where(head, masked[0], masked[3])

    outer = min(4, panels)
    inner = panels // outer
    counts = 4 * ((outer - 1) + (inner - 1) + 1 + (outer - 1) * inner + outer * (inner - 1))
    vmem = pl.BlockSpec(memory_space=pltpu.VMEM)
    own, other = pl.pallas_call(
        functools.partial(kernel, outer, inner, counts),
        out_shape=[jax.ShapeDtypeStruct((2, rows, width), jnp.float32)] * 2,
        in_specs=[vmem] * 4,
        out_specs=[vmem] * 2,
        scratch_shapes=[
            pltpu.VMEM((2, 2, 2, width, width), jnp.bfloat16),
            pltpu.VMEM((2, 2, rows, width), jnp.bfloat16),
            pltpu.VMEM((rows, width), jnp.bfloat16),
            pltpu.VMEM((rows, width), jnp.bfloat16),
            pltpu.VMEM((rows, width), jnp.bfloat16),
            pltpu.SemaphoreType.DMA((2, 2, 2, panels)),
            pltpu.SemaphoreType.DMA((counts,)),
            pltpu.SemaphoreType.DMA((2,)),
            pltpu.SemaphoreType.DMA((2,)),
            pltpu.SemaphoreType.DMA((2, 2)),
            pltpu.SemaphoreType.DMA((2,)),
            pltpu.SemaphoreType.DMA((2,)),
        ],
        compiler_params=pltpu.CompilerParams(
            collective_id=0, has_side_effects=True, vmem_limit_bytes=48 << 20),
        name="merge_levels",
    )(first, second, left, add)
    return jnp.stack([
        jnp.where(head, own[0], other[0]),
        jnp.where(head, own[1], other[1]),
        jnp.where(head, other[1], own[1]),
        jnp.where(head, other[0], own[0]),
    ])[None]


def solution(mesh):
    return jax.shard_map(
        functools.partial(body, mesh.shape["panel"]),
        mesh=mesh,
        in_specs=(P("slab", None, "panel", None), P("slab", None, None, None)),
        out_specs=P("slab", None, "panel", None),
        check_vma=False,
    )
```

```python
import functools
import jax
import jax.numpy as jnp
from jax import lax
from jax.experimental import pallas as pl
from jax.experimental.pallas import tpu as pltpu
from jax.sharding import PartitionSpec as P

BLK = 64
TILE = 256
MESH = pl.DeviceIdType.MESH


def kernel(outer, inner, counts, first_ref, second_ref, left_ref, add_ref, own_ref, other_ref,
           right, swap, base, front, mid, recv_sem, send_sem, swap_recv, swap_send, local_sem, last_recv, last_send):
    rows, width = left_ref.shape
    panels = outer * inner
    slab = lax.axis_index("slab")
    panel = lax.axis_index("panel")
    core = slab % 2
    side = (slab // 2) % 2
    sibling = slab + 1 - 2 * core
    partner = slab + 2 - 4 * side
    out_pos = panel // inner
    in_pos = panel % inner

    column = panel % inner
    rise = panel // inner
    spot_here = column * outer + rise + (outer - 1 - 2 * rise) * (column % 2)

    def at_ring(shift):
        where = (spot_here + shift + panels) % panels
        turn = where // outer
        step = where % outer
        return (step + (outer - 1 - 2 * step) * (turn % 2)) * inner + turn

    ahead = (slab, at_ring(1))
    behind = (slab, at_ring(-1))

    barrier = pltpu.get_barrier_semaphore()
    friends = [ahead, behind, (sibling, panel), (partner, panel)]
    for friend in friends:
        pl.semaphore_signal(barrier, inc=1, device_id=friend, device_id_type=MESH)
    pl.semaphore_wait(barrier, len(friends))

    sent = []
    piece = rows // 2
    reach = panels // 2

    def place(level, kind, owner, p, half):
        return right.at[level, kind, owner, pl.ds(pl.multiple_of(p * rows + half * piece, piece), piece), :]

    def push(level, kind, src, p, half, target, guard):
        spot = len(sent)
        sent.append(guard)
        pltpu.make_async_remote_copy(
            src_ref=src, dst_ref=place(level, kind, core, p, half), send_sem=send_sem.at[spot],
            recv_sem=recv_sem.at[level, kind, core, p, half], device_id=target, device_id_type=MESH).start()

    def arrive(level, kind, owner, p, half):
        spot = place(level, kind, owner, p, half)
        pltpu.make_async_remote_copy(
            src_ref=spot, dst_ref=spot, send_sem=send_sem.at[0], recv_sem=recv_sem.at[level, kind, owner, p, half],
            device_id=(sibling, panel), device_id_type=MESH).wait_recv()

    def share(level, kind, src, p, half, guard):
        if guard == "gives":
            push(level, kind, src, p, half, (partner, panel), guard)
        push(level, kind, src, p, half, (sibling, panel), guard)

    def local_copy(level, kind, src):
        return pltpu.make_async_copy(src, right.at[level, kind, core, pl.ds(pl.multiple_of(panel * rows, rows), rows), :],
                                     local_sem.at[level, kind])

    def open_ring(level, kind, src, guard=None):
        local_copy(level, kind, src).start()
        parts = [src.at[pl.ds(half * piece, piece), :] for half in range(2)]
        for half in range(2):
            push(level, kind, parts[half], panel, half, ahead, guard)
            push(level, kind, parts[half], panel, half, behind, guard)
        for half in range(2):
            share(level, kind, parts[half], panel, half, guard)

    def items(distance):
        for half in range(2):
            for way in (1, -1):
                if distance < reach or (half == 0) == (way == 1):
                    passes = distance + 1 < reach or (distance + 1 == reach and (half == 0) == (way == 1))
                    yield half, way, passes

    def relay(level, kind, distance, guard=None):
        for half, way, passes in items(distance):
            p = at_ring(-way * distance)
            arrive(level, kind, core, p, half)
            src = place(level, kind, core, p, half)
            if passes:
                push(level, kind, src, p, half, ahead if way == 1 else behind, guard)
            share(level, kind, src, p, half, guard)

    def follow(level, kind, distance):
        pairs = [(half, way) for half, way, _ in items(distance)] if distance else [(0, 1), (1, 1)]
        for half, way in pairs:
            p = at_ring(-way * distance)
            arrive(level, kind, core, p, half)
            share(level, kind, place(level, kind, core, p, half), p, half, "takes")

    def settle(level, kind, src, guard=None):
        for distance in range(reach + 1):
            pairs = [(half, way) for half, way, _ in items(distance)] if distance else [(0, 1), (1, 1)]
            for half, way in pairs:
                arrive(level, kind, 1 - core, at_ring(-way * distance), half)
        if guard is None:
            local_copy(level, kind, src).wait()
        else:
            @pl.when(gives == 1)
            def _():
                local_copy(level, kind, src).wait()

    gives = (side + core) % 2
    slot = 1 - gives

    def product(left, factor, emit):
        @pl.loop(0, width // TILE)
        def _(step):
            cols = pl.ds(pl.multiple_of(step * TILE, TILE), TILE)
            emit(cols, jnp.dot(left[...], factor[:, cols], preferred_element_type=jnp.float32))

    def keep(ref):
        def emit(cols, value):
            ref[:, cols] = value.astype(ref.dtype)
        return emit

    def keep_sum(ref, extra):
        def emit(cols, value):
            ref[:, cols] = (extra[:, cols].astype(jnp.float32) + value).astype(ref.dtype)
        return emit

    def swap_copy(kind, which):
        return pltpu.make_async_remote_copy(
            src_ref=swap.at[which, kind], dst_ref=swap.at[which, kind], send_sem=swap_send.at[kind],
            recv_sem=swap_recv.at[kind], device_id=(partner, panel), device_id_type=MESH)

    is_tail = core == 1

    def merge(level, first, second, left, add, outs, after_diag):
        def run(action):
            if level == 0:
                action(None)
            else:
                pl.when(gives == 1)(lambda: action("gives"))

        def step(distance):
            run(lambda guard: relay(level, 1, distance, guard))
            if level == 1:
                pl.when(gives == 0)(lambda: follow(level, 1, distance))

        open_ring(level, 0, first)
        for distance in range(1, reach):
            relay(level, 0, distance)
        run(lambda guard: open_ring(level, 1, second, guard))
        relay(level, 0, reach)
        settle(level, 0, first)
        if level == 1:
            pl.when(gives == 0)(lambda: follow(level, 1, 0))
            pl.when(gives == 1)(lambda: swap_copy(1, 1).wait_recv())
        top = right.at[level, 0, 1 - level]
        bottom = right.at[level, 0, level]

        @pl.when(is_tail)
        def _():
            product(left, bottom, keep(base))

        @pl.when(core == 0)
        def _():
            base[...] = left[...]

        pending = list(range(1, reach + 1))
        early = max(len(pending) // 4, 1)

        def some():
            for _ in range(early):
                if pending:
                    step(pending.pop(0))

        for turn in range(3):
            product(base if turn == 0 else front, top, keep(mid))
            some()
            product(mid, bottom, keep_sum(front, base))
        product(front, top, keep(mid))

        @pl.when(is_tail)
        def _():
            front[...] = (left[...].astype(jnp.float32) + mid[...].astype(jnp.float32)).astype(front.dtype)
            product(mid, bottom, keep_sum(base, base))

        @pl.when(core == 0)
        def _():
            base[...] = mid[...]

        while pending:
            step(pending.pop(0))
        settle(level, 1, second, None if level == 0 else "gives")
        mine = right.at[level, 1, core]
        theirs = right.at[level, 1, 1 - core]
        diag_factor, side_factor = (mine, theirs) if level == 0 else (theirs, mine)
        product(base, diag_factor, keep_sum(outs[0], add))
        after_diag()
        product(front, side_factor, keep(outs[1]))

    merge(0, first_ref, second_ref, left_ref, add_ref,
          (swap.at[slot, 0], swap.at[slot, 1]), lambda: swap_copy(0, slot).start())
    pl.when(gives == 0)(lambda: swap_copy(1, 1).start())
    swap_copy(0, gives).wait_recv()

    def last_copy(kind):
        return pltpu.make_async_remote_copy(
            src_ref=own_ref.at[kind], dst_ref=other_ref.at[kind], send_sem=last_send.at[kind],
            recv_sem=last_recv.at[kind], device_id=(sibling, panel), device_id_type=MESH)

    merge(1, swap.at[0, 0], swap.at[0, 1], swap.at[1, 1], swap.at[1, 0],
          (own_ref.at[0], own_ref.at[1]), lambda: last_copy(0).start())
    last_copy(1).start()
    swap_copy(0, slot).wait_send()
    pl.when(gives == 0)(lambda: swap_copy(1, 1).wait_send())

    def drain(guard):
        own = right.at[0, 0, 0, pl.ds(0, piece), :]
        for spot, kept in enumerate(sent):
            if kept == guard:
                pltpu.make_async_remote_copy(
                    src_ref=own, dst_ref=own, send_sem=send_sem.at[spot], recv_sem=recv_sem.at[0, 0, 0, 0, 0],
                    device_id=(sibling, panel), device_id_type=MESH).wait_send()

    drain(None)
    pl.when(gives == 1)(lambda: drain("gives"))
    pl.when(gives == 0)(lambda: drain("takes"))
    for kind in range(2):
        last_copy(kind).wait()
    assert len(sent) <= counts, len(sent)


def body(panels, ranges, pattern):
    blocks = ranges[0]
    rows, width = blocks.shape[1:]
    count = pattern.shape[2]
    core = lax.axis_index("slab") % 2
    row_start = lax.axis_index("panel") * rows
    row_ids = row_start + jnp.arange(rows, dtype=jnp.int32)
    col_ids = jnp.arange(width, dtype=jnp.int32)
    block_ids = jnp.arange(count, dtype=jnp.int32)
    row_pick = (row_ids[:, None] // BLK == block_ids[None, :]).astype(jnp.float32)
    col_pick = (block_ids[:, None] == col_ids[None, :] // BLK).astype(jnp.float32)
    mask = jnp.einsum("mi,gij,jc->gmc", row_pick, pattern[0].astype(jnp.float32), col_pick)
    masked = blocks * mask
    half = masked.astype(jnp.bfloat16)
    head = core == 0
    first = jnp.where(head, half[3], half[0])
    second = jnp.where(head, half[2], half[1])
    left = jnp.where(head, half[1], half[2])
    add = jnp.where(head, masked[0], masked[3])

    outer = min(4, panels)
    inner = panels // outer
    counts = 20 * panels
    vmem = pl.BlockSpec(memory_space=pltpu.VMEM)
    own, other = pl.pallas_call(
        functools.partial(kernel, outer, inner, counts),
        out_shape=[jax.ShapeDtypeStruct((2, rows, width), jnp.float32)] * 2,
        in_specs=[vmem] * 4,
        out_specs=[vmem] * 2,
        scratch_shapes=[
            pltpu.VMEM((2, 2, 2, width, width), jnp.bfloat16),
            pltpu.VMEM((2, 2, rows, width), jnp.bfloat16),
            pltpu.VMEM((rows, width), jnp.bfloat16),
            pltpu.VMEM((rows, width), jnp.bfloat16),
            pltpu.VMEM((rows, width), jnp.bfloat16),
            pltpu.SemaphoreType.DMA((2, 2, 2, panels, 2)),
            pltpu.SemaphoreType.DMA((counts,)),
            pltpu.SemaphoreType.DMA((2,)),
            pltpu.SemaphoreType.DMA((2,)),
            pltpu.SemaphoreType.DMA((2, 2)),
            pltpu.SemaphoreType.DMA((2,)),
            pltpu.SemaphoreType.DMA((2,)),
        ],
        compiler_params=pltpu.CompilerParams(
            collective_id=0, has_side_effects=True, vmem_limit_bytes=48 << 20),
        name="merge_levels",
    )(first, second, left, add)
    return jnp.stack([
        jnp.where(head, own[0], other[0]),
        jnp.where(head, own[1], other[1]),
        jnp.where(head, other[1], own[1]),
        jnp.where(head, other[0], own[0]),
    ])[None]


def solution(mesh):
    return jax.shard_map(
        functools.partial(body, mesh.shape["panel"]),
        mesh=mesh,
        in_specs=(P("slab", None, "panel", None), P("slab", None, None, None)),
        out_specs=P("slab", None, "panel", None),
        check_vma=False,
    )
```

```python
import functools
import jax
import jax.numpy as jnp
from jax import lax
from jax.experimental import pallas as pl
from jax.experimental.pallas import tpu as pltpu
from jax.sharding import PartitionSpec as P

BLK = 64
TILE = 256
MESH = pl.DeviceIdType.MESH


def kernel(outer, inner, counts, first_ref, second_ref, left_ref, add_ref, own_ref, other_ref,
           right, swap, sums, base, front, mid, recv_sem, send_sem, swap_recv, swap_send, local_sem, last_recv, last_send):
    rows, width = left_ref.shape
    panels = outer * inner
    slab = lax.axis_index("slab")
    panel = lax.axis_index("panel")
    core = slab % 2
    side = (slab // 2) % 2
    sibling = slab + 1 - 2 * core
    partner = slab + 2 - 4 * side
    out_pos = panel // inner
    in_pos = panel % inner

    column = panel % inner
    rise = panel // inner
    spot_here = column * outer + rise + (outer - 1 - 2 * rise) * (column % 2)

    def at_ring(shift):
        where = (spot_here + shift + panels) % panels
        turn = where // outer
        step = where % outer
        return (step + (outer - 1 - 2 * step) * (turn % 2)) * inner + turn

    ahead = (slab, at_ring(1))
    behind = (slab, at_ring(-1))

    barrier = pltpu.get_barrier_semaphore()
    friends = [ahead, behind, (sibling, panel), (partner, panel)]
    for friend in friends:
        pl.semaphore_signal(barrier, inc=1, device_id=friend, device_id_type=MESH)
    pl.semaphore_wait(barrier, len(friends))

    sent = []
    piece = rows // 2
    reach = panels // 2

    def place(level, kind, owner, p, half):
        return right.at[level, kind, owner, pl.ds(pl.multiple_of(p * rows + half * piece, piece), piece), :]

    def push(level, kind, src, p, half, target, guard):
        spot = len(sent)
        sent.append(guard)
        pltpu.make_async_remote_copy(
            src_ref=src, dst_ref=place(level, kind, core, p, half), send_sem=send_sem.at[spot],
            recv_sem=recv_sem.at[level, kind, core, p, half], device_id=target, device_id_type=MESH).start()

    def arrive(level, kind, owner, p, half):
        spot = place(level, kind, owner, p, half)
        pltpu.make_async_remote_copy(
            src_ref=spot, dst_ref=spot, send_sem=send_sem.at[0], recv_sem=recv_sem.at[level, kind, owner, p, half],
            device_id=(sibling, panel), device_id_type=MESH).wait_recv()

    def share(level, kind, src, p, half, guard):
        if guard == "gives" and kind == 1:
            push(level, kind, src, p, half, (partner, panel), guard)
        push(level, kind, src, p, half, (sibling, panel), guard)

    def local_copy(level, kind, src):
        return pltpu.make_async_copy(src, right.at[level, kind, core, pl.ds(pl.multiple_of(panel * rows, rows), rows), :],
                                     local_sem.at[level, kind])

    def open_ring(level, kind, src, guard=None, ready=None):
        for half in range(2):
            if ready:
                ready(half)
            part = src.at[pl.ds(half * piece, piece), :]
            push(level, kind, part, panel, half, ahead, guard)
            push(level, kind, part, panel, half, behind, guard)
            share(level, kind, part, panel, half, guard)
        local_copy(level, kind, src).start()

    def items(distance):
        for half in range(2):
            for way in (1, -1):
                if distance < reach or (half == 0) == (way == 1):
                    passes = distance + 1 < reach or (distance + 1 == reach and (half == 0) == (way == 1))
                    yield half, way, passes

    def relay(level, kind, distance, guard=None):
        for half, way, passes in items(distance):
            p = at_ring(-way * distance)
            arrive(level, kind, core, p, half)
            src = place(level, kind, core, p, half)
            if passes:
                push(level, kind, src, p, half, ahead if way == 1 else behind, guard)
            share(level, kind, src, p, half, guard)

    def follow(level, kind, distance):
        pairs = [(half, way) for half, way, _ in items(distance)] if distance else [(0, 1), (1, 1)]
        for half, way in pairs:
            p = at_ring(-way * distance)
            arrive(level, kind, core, p, half)
            share(level, kind, place(level, kind, core, p, half), p, half, "takes")

    def settle(level, kind, distances):
        for distance in distances:
            pairs = [(half, way) for half, way, _ in items(distance)] if distance else [(0, 1), (1, 1)]
            for half, way in pairs:
                arrive(level, kind, 1 - core, at_ring(-way * distance), half)

    gives = (side + core) % 2
    slot = 1 - gives

    def product(left, factor, emit):
        @pl.loop(0, width // TILE)
        def _(step):
            cols = pl.ds(pl.multiple_of(step * TILE, TILE), TILE)
            emit(cols, jnp.dot(left[...], factor[:, cols], preferred_element_type=jnp.float32))

    def keep(ref):
        def emit(cols, value):
            ref[:, cols] = value.astype(ref.dtype)
        return emit

    def keep_sum(ref, extra):
        def emit(cols, value):
            ref[:, cols] = (extra[:, cols].astype(jnp.float32) + value).astype(ref.dtype)
        return emit

    def swap_copy(which):
        ref = swap.at[0, 0, pl.ds(which * piece, piece), :] if which < 2 else swap.at[1, 3 - which]
        return pltpu.make_async_remote_copy(
            src_ref=ref, dst_ref=ref, send_sem=swap_send.at[which],
            recv_sem=swap_recv.at[which], device_id=(partner, panel), device_id_type=MESH)

    is_tail = core == 1

    def merge(level, lead, first, second, left, add, outs, after_diag):
        def run(action):
            if level == 0:
                action(None)
            else:
                pl.when(gives == 1)(lambda: action("gives"))

        def step(distance):
            run(lambda guard: relay(level, 1, distance, guard))
            if level == 1:
                pl.when(gives == 0)(lambda: follow(level, 1, distance))

        split = rows % 128 == 0
        if level == 0:
            open_ring(level, 0, first)
        for distance in range(1, reach):
            relay(level, 0, distance)
            if distance == lead:
                run(lambda guard: open_ring(level, 1, second, guard))
                if level == 1:
                    pl.when(gives == 0)(lambda: follow(level, 1, 0))
            if distance > lead:
                step(distance - lead)
        relay(level, 0, reach)
        settle(level, 0, range(reach + 1))
        local_copy(level, 0, first).wait()
        if level == 1:
            pl.when(gives == 1)(lambda: swap_copy(2).wait_recv())
        top = right.at[level, 0, 1 - level]
        bottom = right.at[level, 0, level]

        @pl.when(is_tail)
        def _():
            product(left, bottom, keep(base))

        @pl.when(core == 0)
        def _():
            base[...] = left[...]

        pending = list(range(max(reach - lead, 1), reach + 1))
        last = [pending.pop()] if split else []
        early = max(len(pending) // 4, 1)

        def some():
            for _ in range(early):
                if pending:
                    step(pending.pop(0))

        for turn in range(3):
            product(base if turn == 0 else front, top, keep(mid))
            some()
            product(mid, bottom, keep_sum(front, base))
        product(front, top, keep(mid))

        @pl.when(is_tail)
        def _():
            front[...] = (left[...].astype(jnp.float32) + mid[...].astype(jnp.float32)).astype(front.dtype)
            product(mid, bottom, keep_sum(base, base))

        @pl.when(core == 0)
        def _():
            base[...] = mid[...]

        mine = right.at[level, 1, core]
        theirs = right.at[level, 1, 1 - core]
        diag_factor, side_factor = (mine, theirs) if level == 0 else (theirs, mine)
        while pending:
            step(pending.pop(0))
        settle(level, 1, range(reach if split else reach + 1))
        run(lambda guard: local_copy(level, 1, second).wait())

        def term(left, factor, cols, p):
            span = pl.ds(pl.multiple_of(p * rows, rows), rows)
            return jnp.dot(left[:, span], factor[span, cols], preferred_element_type=jnp.float32)

        near = [0] + [way * distance for distance in range(1, reach) for way in (1, -1)]

        def partial(left, factor, out):
            @pl.loop(0, width // TILE)
            def _(tile):
                cols = pl.ds(pl.multiple_of(tile * TILE, TILE), TILE)
                out[:, cols] = sum(term(left, factor, cols, at_ring(shift)) for shift in near)

        def finish(left, factor, part, emit):
            @pl.loop(0, width // TILE)
            def _(tile):
                cols = pl.ds(pl.multiple_of(tile * TILE, TILE), TILE)
                emit(cols, part[:, cols] + term(left, factor, cols, at_ring(reach)))

        if split:
            partial(base, diag_factor, sums.at[0])
            partial(front, side_factor, sums.at[1])
            step(last[0])
            settle(level, 1, [reach])
        if level == 1:
            pl.when(gives == 1)(lambda: swap_copy(3).wait_recv())
        if split:
            finish(base, diag_factor, sums.at[0], keep_sum(outs[0], add))
            after_diag()
            finish(front, side_factor, sums.at[1], keep(outs[1]))
        else:
            product(base, diag_factor, keep_sum(outs[0], add))
            after_diag()
            product(front, side_factor, keep(outs[1]))

    def give():
        for half in range(2):
            swap_copy(half).start()
        open_ring(1, 0, swap.at[0, 0], "gives")

    def take():
        swap_copy(2).start()
        open_ring(1, 0, swap.at[0, 0], "takes", lambda half: swap_copy(half).wait_recv())
        swap_copy(3).start()

    merge(0, max(reach - 1, 1), first_ref, second_ref, left_ref, add_ref,
          (swap.at[slot, 0], swap.at[slot, 1]), lambda: pl.when(gives == 1)(give))
    pl.when(gives == 0)(take)

    def last_copy(kind):
        return pltpu.make_async_remote_copy(
            src_ref=own_ref.at[kind], dst_ref=other_ref.at[kind], send_sem=last_send.at[kind],
            recv_sem=last_recv.at[kind], device_id=(sibling, panel), device_id_type=MESH)

    merge(1, 1, swap.at[0, 0], swap.at[0, 1], swap.at[1, 1], swap.at[1, 0],
          (own_ref.at[0], own_ref.at[1]), lambda: last_copy(0).start())
    last_copy(1).start()

    @pl.when(gives == 1)
    def _():
        for which in (0, 1):
            swap_copy(which).wait_send()

    @pl.when(gives == 0)
    def _():
        for which in (2, 3):
            swap_copy(which).wait_send()

    def drain(guard):
        own = right.at[0, 0, 0, pl.ds(0, piece), :]
        for spot, kept in enumerate(sent):
            if kept == guard:
                pltpu.make_async_remote_copy(
                    src_ref=own, dst_ref=own, send_sem=send_sem.at[spot], recv_sem=recv_sem.at[0, 0, 0, 0, 0],
                    device_id=(sibling, panel), device_id_type=MESH).wait_send()

    drain(None)
    pl.when(gives == 1)(lambda: drain("gives"))
    pl.when(gives == 0)(lambda: drain("takes"))
    for kind in range(2):
        last_copy(kind).wait()
    assert len(sent) <= counts, len(sent)


def body(panels, ranges, pattern):
    blocks = ranges[0]
    rows, width = blocks.shape[1:]
    count = pattern.shape[2]
    core = lax.axis_index("slab") % 2
    row_start = lax.axis_index("panel") * rows
    row_ids = row_start + jnp.arange(rows, dtype=jnp.int32)
    col_ids = jnp.arange(width, dtype=jnp.int32)
    block_ids = jnp.arange(count, dtype=jnp.int32)
    row_pick = (row_ids[:, None] // BLK == block_ids[None, :]).astype(jnp.float32)
    col_pick = (block_ids[:, None] == col_ids[None, :] // BLK).astype(jnp.float32)
    mask = jnp.einsum("mi,gij,jc->gmc", row_pick, pattern[0].astype(jnp.float32), col_pick)
    masked = blocks * mask
    half = masked.astype(jnp.bfloat16)
    head = core == 0
    first = jnp.where(head, half[3], half[0])
    second = jnp.where(head, half[2], half[1])
    left = jnp.where(head, half[1], half[2])
    add = jnp.where(head, masked[0], masked[3])

    outer = min(4, panels)
    inner = panels // outer
    counts = 24 * panels
    vmem = pl.BlockSpec(memory_space=pltpu.VMEM)
    own, other = pl.pallas_call(
        functools.partial(kernel, outer, inner, counts),
        out_shape=[jax.ShapeDtypeStruct((2, rows, width), jnp.float32)] * 2,
        in_specs=[vmem] * 4,
        out_specs=[vmem] * 2,
        scratch_shapes=[
            pltpu.VMEM((2, 2, 2, width, width), jnp.bfloat16),
            pltpu.VMEM((2, 2, rows, width), jnp.bfloat16),
            pltpu.VMEM((2, rows, width), jnp.float32),
            pltpu.VMEM((rows, width), jnp.bfloat16),
            pltpu.VMEM((rows, width), jnp.bfloat16),
            pltpu.VMEM((rows, width), jnp.bfloat16),
            pltpu.SemaphoreType.DMA((2, 2, 2, panels, 2)),
            pltpu.SemaphoreType.DMA((counts,)),
            pltpu.SemaphoreType.DMA((4,)),
            pltpu.SemaphoreType.DMA((4,)),
            pltpu.SemaphoreType.DMA((2, 2)),
            pltpu.SemaphoreType.DMA((2,)),
            pltpu.SemaphoreType.DMA((2,)),
        ],
        compiler_params=pltpu.CompilerParams(
            collective_id=0, has_side_effects=True, vmem_limit_bytes=48 << 20),
        name="merge_levels",
    )(first, second, left, add)
    return jnp.stack([
        jnp.where(head, own[0], other[0]),
        jnp.where(head, own[1], other[1]),
        jnp.where(head, other[1], own[1]),
        jnp.where(head, other[0], own[0]),
    ])[None]


def solution(mesh):
    return jax.shard_map(
        functools.partial(body, mesh.shape["panel"]),
        mesh=mesh,
        in_specs=(P("slab", None, "panel", None), P("slab", None, None, None)),
        out_specs=P("slab", None, "panel", None),
        check_vma=False,
    )
```

```python
import functools
import jax
import jax.numpy as jnp
from jax import lax
from jax.experimental import pallas as pl
from jax.experimental.pallas import tpu as pltpu
from jax.sharding import PartitionSpec as P

BLK = 64
MESH = pl.DeviceIdType.MESH


def kernel(outer, inner, counts, first_ref, second_ref, left_ref, add_ref, own_ref, other_ref,
           right, swap, sums, base, front, mid, recv_sem, send_sem, swap_recv, swap_send, local_sem, last_recv, last_send):
    rows, width = left_ref.shape
    panels = outer * inner
    slab = lax.axis_index("slab")
    panel = lax.axis_index("panel")
    core = slab % 2
    side = (slab // 2) % 2
    sibling = slab + 1 - 2 * core
    partner = slab + 2 - 4 * side
    out_pos = panel // inner
    in_pos = panel % inner

    column = panel % inner
    rise = panel // inner
    spot_here = column * outer + rise + (outer - 1 - 2 * rise) * (column % 2)

    def at_ring(shift):
        where = (spot_here + shift + panels) % panels
        turn = where // outer
        step = where % outer
        return (step + (outer - 1 - 2 * step) * (turn % 2)) * inner + turn

    ahead = (slab, at_ring(1))
    behind = (slab, at_ring(-1))

    barrier = pltpu.get_barrier_semaphore()
    friends = [ahead, behind, (sibling, panel), (partner, panel)]
    for friend in friends:
        pl.semaphore_signal(barrier, inc=1, device_id=friend, device_id_type=MESH)
    pl.semaphore_wait(barrier, len(friends))

    sent = []
    piece = rows // 2
    reach = panels // 2

    def place(level, kind, owner, p, half):
        return right.at[level, kind, owner, pl.ds(pl.multiple_of(p * rows + half * piece, piece), piece), :]

    def push(level, kind, src, p, half, target, guard):
        spot = len(sent)
        sent.append(guard)
        pltpu.make_async_remote_copy(
            src_ref=src, dst_ref=place(level, kind, core, p, half), send_sem=send_sem.at[spot],
            recv_sem=recv_sem.at[level, kind, core, p, half], device_id=target, device_id_type=MESH).start()

    def arrive(level, kind, owner, p, half):
        spot = place(level, kind, owner, p, half)
        pltpu.make_async_remote_copy(
            src_ref=spot, dst_ref=spot, send_sem=send_sem.at[0], recv_sem=recv_sem.at[level, kind, owner, p, half],
            device_id=(sibling, panel), device_id_type=MESH).wait_recv()

    def share(level, kind, src, p, half, guard):
        if guard == "gives" and kind == 1:
            push(level, kind, src, p, half, (partner, panel), guard)
        push(level, kind, src, p, half, (sibling, panel), guard)

    def local_copy(level, kind, src):
        return pltpu.make_async_copy(src, right.at[level, kind, core, pl.ds(pl.multiple_of(panel * rows, rows), rows), :],
                                     local_sem.at[level, kind])

    def open_ring(level, kind, src, guard=None, ready=None):
        for half in range(2):
            if ready:
                ready(half)
            part = src.at[pl.ds(half * piece, piece), :]
            push(level, kind, part, panel, half, ahead, guard)
            push(level, kind, part, panel, half, behind, guard)
            share(level, kind, part, panel, half, guard)
        local_copy(level, kind, src).start()

    def items(distance):
        for half in range(2):
            for way in (1, -1):
                if distance < reach or (half == 0) == (way == 1):
                    passes = distance + 1 < reach or (distance + 1 == reach and (half == 0) == (way == 1))
                    yield half, way, passes

    def relay(level, kind, distance, guard=None):
        for half, way, passes in items(distance):
            p = at_ring(-way * distance)
            arrive(level, kind, core, p, half)
            src = place(level, kind, core, p, half)
            if passes:
                push(level, kind, src, p, half, ahead if way == 1 else behind, guard)
            share(level, kind, src, p, half, guard)

    def follow(level, kind, distance):
        pairs = [(half, way) for half, way, _ in items(distance)] if distance else [(0, 1), (1, 1)]
        for half, way in pairs:
            p = at_ring(-way * distance)
            arrive(level, kind, core, p, half)
            share(level, kind, place(level, kind, core, p, half), p, half, "takes")

    def settle(level, kind, distances):
        for distance in distances:
            pairs = [(half, way) for half, way, _ in items(distance)] if distance else [(0, 1), (1, 1)]
            for half, way in pairs:
                arrive(level, kind, 1 - core, at_ring(-way * distance), half)

    gives = (side + core) % 2
    slot = 1 - gives

    def product(left, factor, emit):
        @pl.loop(0, width // width)
        def _(step):
            cols = pl.ds(pl.multiple_of(step * width, width), width)
            emit(cols, jnp.dot(left[...], factor[:, cols], preferred_element_type=jnp.float32))

    def keep(ref):
        def emit(cols, value):
            ref[:, cols] = value.astype(ref.dtype)
        return emit

    def keep_sum(ref, extra):
        def emit(cols, value):
            ref[:, cols] = (extra[:, cols].astype(jnp.float32) + value).astype(ref.dtype)
        return emit

    def swap_copy(which):
        ref = swap.at[0, 0, pl.ds(which * piece, piece), :] if which < 2 else swap.at[1, 3 - which]
        return pltpu.make_async_remote_copy(
            src_ref=ref, dst_ref=ref, send_sem=swap_send.at[which],
            recv_sem=swap_recv.at[which], device_id=(partner, panel), device_id_type=MESH)

    is_tail = core == 1

    def merge(level, lead, first, second, left, add, outs, after_diag):
        def run(action):
            if level == 0:
                action(None)
            else:
                pl.when(gives == 1)(lambda: action("gives"))

        def step(distance):
            run(lambda guard: relay(level, 1, distance, guard))
            if level == 1:
                pl.when(gives == 0)(lambda: follow(level, 1, distance))

        def start_second():
            run(lambda guard: open_ring(level, 1, second, guard))
            if level == 1:
                pl.when(gives == 0)(lambda: follow(level, 1, 0))

        split = rows % 128 == 0
        if level == 0:
            open_ring(level, 0, first)
        if lead == 0:
            start_second()
        for distance in range(1, reach):
            relay(level, 0, distance)
            if distance == lead:
                start_second()
            if distance > lead:
                step(distance - lead)
        relay(level, 0, reach)
        settle(level, 0, range(reach + 1))
        local_copy(level, 0, first).wait()
        if level == 1:
            pl.when(gives == 1)(lambda: swap_copy(2).wait_recv())
        top = right.at[level, 0, 1 - level]
        bottom = right.at[level, 0, level]

        @pl.when(is_tail)
        def _():
            product(left, bottom, keep(base))

        @pl.when(core == 0)
        def _():
            base[...] = left[...]

        pending = list(range(max(reach - lead, 1), reach + 1))
        last = [pending.pop()] if split else []
        early = max(len(pending) // 4, 1)

        def some():
            for _ in range(early):
                if pending:
                    step(pending.pop(0))

        for turn in range(3):
            product(base if turn == 0 else front, top, keep(mid))
            some()
            product(mid, bottom, keep_sum(front, base))
        product(front, top, keep(mid))

        @pl.when(is_tail)
        def _():
            front[...] = (left[...].astype(jnp.float32) + mid[...].astype(jnp.float32)).astype(front.dtype)
            product(mid, bottom, keep_sum(base, base))

        @pl.when(core == 0)
        def _():
            base[...] = mid[...]

        mine = right.at[level, 1, core]
        theirs = right.at[level, 1, 1 - core]
        diag_factor, side_factor = (mine, theirs) if level == 0 else (theirs, mine)
        while pending:
            step(pending.pop(0))
        settle(level, 1, range(reach if split else reach + 1))
        run(lambda guard: local_copy(level, 1, second).wait())

        def term(left, factor, cols, p):
            span = pl.ds(pl.multiple_of(p * rows, rows), rows)
            return jnp.dot(left[:, span], factor[span, cols], preferred_element_type=jnp.float32)

        near = [0] + [way * distance for distance in range(1, reach) for way in (1, -1)]

        def partial(left, factor, out):
            @pl.loop(0, width // width)
            def _(tile):
                cols = pl.ds(pl.multiple_of(tile * width, width), width)
                out[:, cols] = sum(term(left, factor, cols, at_ring(shift)) for shift in near)

        def finish(left, factor, part, emit):
            @pl.loop(0, width // width)
            def _(tile):
                cols = pl.ds(pl.multiple_of(tile * width, width), width)
                emit(cols, part[:, cols] + term(left, factor, cols, at_ring(reach)))

        if split:
            partial(base, diag_factor, sums.at[0])
            partial(front, side_factor, sums.at[1])
            step(last[0])
            settle(level, 1, [reach])
        if level == 1:
            pl.when(gives == 1)(lambda: swap_copy(3).wait_recv())
        if split:
            finish(base, diag_factor, sums.at[0], keep_sum(outs[0], add))
            after_diag()
            finish(front, side_factor, sums.at[1], keep(outs[1]))
        else:
            product(base, diag_factor, keep_sum(outs[0], add))
            after_diag()
            product(front, side_factor, keep(outs[1]))

    def give():
        for half in range(2):
            swap_copy(half).start()
        open_ring(1, 0, swap.at[0, 0], "gives")

    def take():
        swap_copy(2).start()
        open_ring(1, 0, swap.at[0, 0], "takes", lambda half: swap_copy(half).wait_recv())
        swap_copy(3).start()

    merge(0, 1, first_ref, second_ref, left_ref, add_ref,
          (swap.at[slot, 0], swap.at[slot, 1]), lambda: pl.when(gives == 1)(give))
    pl.when(gives == 0)(take)

    def last_copy(kind):
        return pltpu.make_async_remote_copy(
            src_ref=own_ref.at[kind], dst_ref=other_ref.at[kind], send_sem=last_send.at[kind],
            recv_sem=last_recv.at[kind], device_id=(sibling, panel), device_id_type=MESH)

    merge(1, 0, swap.at[0, 0], swap.at[0, 1], swap.at[1, 1], swap.at[1, 0],
          (own_ref.at[0], own_ref.at[1]), lambda: last_copy(0).start())
    last_copy(1).start()

    @pl.when(gives == 1)
    def _():
        for which in (0, 1):
            swap_copy(which).wait_send()

    @pl.when(gives == 0)
    def _():
        for which in (2, 3):
            swap_copy(which).wait_send()

    def drain(guard):
        own = right.at[0, 0, 0, pl.ds(0, piece), :]
        for spot, kept in enumerate(sent):
            if kept == guard:
                pltpu.make_async_remote_copy(
                    src_ref=own, dst_ref=own, send_sem=send_sem.at[spot], recv_sem=recv_sem.at[0, 0, 0, 0, 0],
                    device_id=(sibling, panel), device_id_type=MESH).wait_send()

    drain(None)
    pl.when(gives == 1)(lambda: drain("gives"))
    pl.when(gives == 0)(lambda: drain("takes"))
    for kind in range(2):
        last_copy(kind).wait()
    assert len(sent) <= counts, len(sent)


def body(panels, ranges, pattern):
    blocks = ranges[0]
    rows, width = blocks.shape[1:]
    count = pattern.shape[2]
    core = lax.axis_index("slab") % 2
    row_start = lax.axis_index("panel") * rows
    row_ids = row_start + jnp.arange(rows, dtype=jnp.int32)
    col_ids = jnp.arange(width, dtype=jnp.int32)
    block_ids = jnp.arange(count, dtype=jnp.int32)
    row_pick = (row_ids[:, None] // BLK == block_ids[None, :]).astype(jnp.float32)
    col_pick = (block_ids[:, None] == col_ids[None, :] // BLK).astype(jnp.float32)
    mask = jnp.einsum("mi,gij,jc->gmc", row_pick, pattern[0].astype(jnp.float32), col_pick)
    masked = blocks * mask
    half = masked.astype(jnp.bfloat16)
    head = core == 0
    first = jnp.where(head, half[3], half[0])
    second = jnp.where(head, half[2], half[1])
    left = jnp.where(head, half[1], half[2])
    add = jnp.where(head, masked[0], masked[3])

    outer = min(4, panels)
    inner = panels // outer
    counts = 24 * panels
    vmem = pl.BlockSpec(memory_space=pltpu.VMEM)
    own, other = pl.pallas_call(
        functools.partial(kernel, outer, inner, counts),
        out_shape=[jax.ShapeDtypeStruct((2, rows, width), jnp.float32)] * 2,
        in_specs=[vmem] * 4,
        out_specs=[vmem] * 2,
        scratch_shapes=[
            pltpu.VMEM((2, 2, 2, width, width), jnp.bfloat16),
            pltpu.VMEM((2, 2, rows, width), jnp.bfloat16),
            pltpu.VMEM((2, rows, width), jnp.float32),
            pltpu.VMEM((rows, width), jnp.bfloat16),
            pltpu.VMEM((rows, width), jnp.bfloat16),
            pltpu.VMEM((rows, width), jnp.bfloat16),
            pltpu.SemaphoreType.DMA((2, 2, 2, panels, 2)),
            pltpu.SemaphoreType.DMA((counts,)),
            pltpu.SemaphoreType.DMA((4,)),
            pltpu.SemaphoreType.DMA((4,)),
            pltpu.SemaphoreType.DMA((2, 2)),
            pltpu.SemaphoreType.DMA((2,)),
            pltpu.SemaphoreType.DMA((2,)),
        ],
        compiler_params=pltpu.CompilerParams(
            collective_id=0, has_side_effects=True, vmem_limit_bytes=48 << 20),
        name="merge_levels",
    )(first, second, left, add)
    return jnp.stack([
        jnp.where(head, own[0], other[0]),
        jnp.where(head, own[1], other[1]),
        jnp.where(head, other[1], own[1]),
        jnp.where(head, other[0], own[0]),
    ])[None]


def solution(mesh):
    return jax.shard_map(
        functools.partial(body, mesh.shape["panel"]),
        mesh=mesh,
        in_specs=(P("slab", None, "panel", None), P("slab", None, None, None)),
        out_specs=P("slab", None, "panel", None),
        check_vma=False,
    )
```
